128 devices in a mesh: ctx: 16 (over x, y_lo, core), ch: 8 (over y_hi, z).
Axes of the slice: x: 4, y: 4 (y_hi: 2, y_lo: 2; y = y_hi * 2 + y_lo), z: 4, core: 2. Of those that a mesh axis runs over, the one named last changes fastest.
Arguments:
- query_in: bfloat16 [3072, 8192], P('ctx', 'ch'), may hold values from -6 to 6
- key_in: bfloat16 [3072, 8192], P('ctx', 'ch'), may hold values from -6 to 6
- value_in: bfloat16 [3072, 8192], P('ctx', 'ch'), may hold values from -6 to 6
- filters: bfloat16 [512, 3072], P('ch'), may hold values from -0.8 to 0.8
- skip_gain: float32 [8192], P('ch'), may hold values from -3 to 3
- out_weight: bfloat16 [8192, 8192], P(None, 'ch'), may hold values from -0.0625 to 0.0625
Outputs:
- output: bfloat16 [3072, 8192], P('ctx', 'ch')
The draws below stay inside these ranges and needn't reach their ends.
All inputs are finite; a program needn't handle non-finite values.
Results may differ from the reference program's by a relative error of at most 0.0057.
Values may be sent and summed in bfloat16 or wider, within the bound.
No kernel may reach another device: no remote copies, remote signals or barrier semaphores. Data moves between devices by JAX's collectives and lax.ppermute only.
A program may use at most 128 MiB of HBM per device.

```python
import jax
import jax.numpy as jnp

D = 8192
CG = 16
SEQ = 3072
G = 512


def draw_filters(key, part):
    first, second = jax.random.split(key, 2)
    lowest = 30.0
    spans = jnp.exp(jax.random.uniform(first, (G, 1), jnp.float32, jnp.log(lowest), jnp.log(3.0 * SEQ)))
    lags = jnp.arange(SEQ).astype(jnp.float32)[None, :]
    envelope = jnp.exp(-lags / spans) * jnp.sqrt(2.0 / jnp.minimum(spans, SEQ * 1.0))
    noise = jnp.clip(jax.random.normal(second, (G, SEQ), jnp.float32), -3.0, 3.0)
    return (envelope * noise).astype(jnp.bfloat16)


def shard_levels(rng, dims, shards, least, largest):
    def one(position, blocks):
        steps = jax.random.uniform(jax.random.fold_in(jax.random.fold_in(rng, 6), position), (blocks,), jnp.float32, least / len(shards), largest / len(shards))
        return jnp.repeat(jnp.exp(steps), dims[position] // blocks).reshape((-1,) + (1,) * (len(dims) - position - 1))

    loudness = one(*shards[0])
    for cut in shards[1:]:
        loudness = loudness * one(*cut)
    return loudness


def gaussian(stream_key, extent, deviation, limit, pieces=(), dtype=jnp.bfloat16):
    result = deviation * jax.random.normal(stream_key, extent, jnp.float32)
    if pieces:
        result = result * shard_levels(stream_key, extent, pieces, -0.22, 0.18)
    return jnp.clip(result, -limit, limit).astype(dtype)


def setup_inputs(seed: int = 0) -> dict:
    key_list = jax.random.split(jax.random.key(seed), 7)
    query_in = gaussian(key_list[0], (SEQ, D), 1.0, 6.0, ((0, 16), (1, 8)))
    key_in = gaussian(key_list[1], (SEQ, D), 1.0, 6.0, ((0, 16), (1, 8)))
    value_in = gaussian(key_list[2], (SEQ, D), 1.0, 6.0, ((0, 16), (1, 8)))
    filters = draw_filters(jax.random.fold_in(key_list[6], 71), 0)
    skip_gain = gaussian(key_list[4], (D,), 0.5, 3.0, ((0, 8),), jnp.float32)
    out_weight = gaussian(key_list[5], (D, D), D ** -0.5, 0.0625, ((1, 8),))
    return dict(query_in=query_in, key_in=key_in, value_in=value_in, filters=filters, skip_gain=skip_gain, out_weight=out_weight)


def reference(query_in, key_in, value_in, filters, skip_gain, out_weight):
    mixed = (key_in.astype(jnp.float32) * value_in.astype(jnp.float32)).astype(jnp.bfloat16)
    signal = mixed.astype(jnp.float32).T.reshape(G, CG, SEQ)
    spectrum = jnp.fft.rfft(signal, n=2 * SEQ, axis=-1)
    response = jnp.fft.rfft(filters.astype(jnp.float32), n=2 * SEQ, axis=-1)[:, None, :]
    conv = jnp.fft.irfft(spectrum * response, n=2 * SEQ, axis=-1)[..., :SEQ]
    conv = conv.reshape(D, SEQ).T.astype(jnp.float32)
    direct = skip_gain.astype(jnp.float32)[None, :] * mixed.astype(jnp.float32)
    gated = (query_in.astype(jnp.float32) * (conv + direct)).astype(jnp.bfloat16)
    return jnp.dot(gated, out_weight, preferred_element_type=jnp.float32).astype(jnp.bfloat16)
```

```python
import functools

import jax
import jax.numpy as jnp
from jax import lax
from jax.experimental import pallas as pl
from jax.experimental.pallas import tpu as pltpu
from jax.sharding import Mesh, PartitionSpec as P

CTX = ("x", "ylo", "core")
CH = ("yhi", "z")
FRONT = 256
BACK = 128
NT = (((1,), (1,)), ((), ()))


def identity(size):
    rows = lax.broadcasted_iota(jnp.int32, (size, size), 0)
    columns = lax.broadcasted_iota(jnp.int32, (size, size), 1)
    return (rows == columns).astype(jnp.bfloat16)


def mix_kernel(key_ref, value_ref, out_ref):
    product = key_ref[...].astype(jnp.float32) * value_ref[...].astype(jnp.float32)
    mixed = product.astype(jnp.bfloat16)
    width = mixed.shape[1]
    turned = lax.dot_general(identity(width), mixed, NT, preferred_element_type=jnp.float32)
    out_ref[...] = turned.astype(jnp.bfloat16)


def mix(key_in, value_in):
    rows, channels = key_in.shape
    step = 256
    block = pl.BlockSpec((rows, step), lambda n: (0, n))
    return pl.pallas_call(
        mix_kernel,
        grid=(channels // step,),
        out_shape=jax.ShapeDtypeStruct((channels, rows), jnp.bfloat16),
        in_specs=[block, block],
        out_specs=pl.BlockSpec((step, rows), lambda n: (n, 0)),
        name="mix",
    )(key_in, value_in)


def conv_kernel(x_ref, filters_ref, out_ref, shifted_ref, acc_ref):
    blocks, per_group, rows = x_ref.shape
    groups, seq = filters_ref.shape
    ctx = (lax.axis_index("x") * 2 + lax.axis_index("ylo")) * 2 + lax.axis_index("core")
    group = ctx * pl.num_programs(0) + pl.program_id(0)
    tall = 16
    pick = lax.broadcasted_iota(jnp.int32, (tall, groups), 1) == group
    taps = jnp.dot(
        pick.astype(jnp.bfloat16), filters_ref[...], preferred_element_type=jnp.float32
    )
    line = jnp.concatenate(
        [jnp.zeros((tall, FRONT), jnp.float32), taps, jnp.zeros((tall, BACK), jnp.float32)], axis=1
    )
    row = lax.broadcasted_iota(jnp.int32, line.shape, 0)
    for bit in (1, 2, 4, 8):
        line = jnp.where((row & bit) != 0, pltpu.roll(line, bit, 1), line)
    for shift in range(8):
        moved = line if shift == 0 else pltpu.roll(line, 16 * shift, 1)
        shifted_ref[shift] = moved.astype(jnp.bfloat16)
    acc_ref[...] = jnp.zeros_like(acc_ref)
    source = x_ref[...].reshape(blocks * per_group, rows)
    for lag in range(blocks):
        parts = []
        for k in range(rows // 16):
            offset = FRONT + rows * lag - 16 * k
            shift = (-offset // 16) % 8
            start = offset + 16 * shift
            parts.append(shifted_ref[shift, :, start : start + rows])
        tile = jnp.concatenate(parts, axis=0)
        height = (blocks - lag) * per_group
        acc_ref[lag * per_group :, :] += jnp.dot(
            source[:height], tile, preferred_element_type=jnp.float32
        )
    out_ref[...] = acc_ref[...].astype(jnp.bfloat16).reshape(blocks, per_group, rows)


def convolve(x, filters):
    blocks, channels, rows = x.shape
    seq = filters.shape[1]
    per_group = 16
    block = pl.BlockSpec((blocks, per_group, rows), lambda g: (0, g, 0))
    return pl.pallas_call(
        conv_kernel,
        grid=(channels // per_group,),
        out_shape=jax.ShapeDtypeStruct(x.shape, jnp.bfloat16),
        in_specs=[block, pl.BlockSpec(filters.shape, lambda g: (0, 0))],
        out_specs=block,
        scratch_shapes=[
            pltpu.VMEM((8, 16, FRONT + seq + BACK), jnp.bfloat16),
            pltpu.VMEM((blocks * per_group, rows), jnp.float32),
        ],
        name="conv",
    )(x, filters)


def gate_kernel(conv_ref, query_ref, key_ref, value_ref, gain_ref, out_ref):
    rows = query_ref.shape[0]
    conv = lax.dot_general(identity(rows), conv_ref[...], NT, preferred_element_type=jnp.float32)
    product = key_ref[...].astype(jnp.float32) * value_ref[...].astype(jnp.float32)
    mixed = product.astype(jnp.bfloat16).astype(jnp.float32)
    total = conv + gain_ref[...] * mixed
    out_ref[...] = (query_ref[...].astype(jnp.float32) * total).astype(jnp.bfloat16)


def gate(conv, query_in, key_in, value_in, gain):
    rows, channels = query_in.shape
    step = 256
    block = pl.BlockSpec((rows, step), lambda n: (0, n))
    return pl.pallas_call(
        gate_kernel,
        grid=(channels // step,),
        out_shape=jax.ShapeDtypeStruct((rows, channels), jnp.bfloat16),
        in_specs=[
            pl.BlockSpec((step, rows), lambda n: (n, 0)),
            block,
            block,
            block,
            pl.BlockSpec((1, step), lambda n: (0, n)),
        ],
        out_specs=block,
        name="gate",
    )(conv, query_in, key_in, value_in, gain)


def ring(size, step):
    return [(i, (i + step) % size) for i in range(size)]


def gather_project(gated, out_weight):
    depth = gated.shape[1]
    yhi = lax.axis_index("yhi")
    z = lax.axis_index("z")

    def along(block, step):
        return lax.ppermute(block, "z", ring(4, step))

    def across(block):
        return lax.ppermute(block, "yhi", ring(2, 1))

    def term(block, side, back):
        owner = (yhi ^ side) * 4 + (z + 4 - back) % 4
        part = lax.dynamic_slice_in_dim(out_weight, owner * depth, depth, 0)
        return jnp.dot(block, part, preferred_element_type=jnp.float32)

    own = {0: gated}
    for step in (1, 3, 2):
        own[step] = along(gated, step)
    other = {0: across(gated)}
    for step in (1, 3):
        other[step] = along(other[0], step)
    other[2] = across(own[2])
    total = term(own[0], 0, 0)
    for step in (1, 3, 2):
        total = total + term(own[step], 0, step)
    for step in (0, 1, 3, 2):
        total = total + term(other[step], 1, step)
    return total.astype(jnp.bfloat16)


def shards(query_in, key_in, value_in, filters, skip_gain, out_weight):
    rows, channels = query_in.shape
    mixed = mix(key_in, value_in)
    sent = mixed.reshape(16, channels // 16, rows)
    whole = lax.all_to_all(sent, CTX, 0, 0, tiled=True)
    conv = convolve(whole, filters)
    back = lax.all_to_all(conv, CTX, 0, 0, tiled=True)
    gated = gate(
        back.reshape(channels, rows), query_in, key_in, value_in, skip_gain.reshape(1, channels)
    )
    return gather_project(gated, out_weight)


def solution(mesh):
    fine = Mesh(mesh.devices.reshape(4, 2, 2, 2, 4), CTX + CH)
    placed = (P(CTX, CH), P(CTX, CH), P(CTX, CH), P(CH, None), P(CH), P(None, CH))
    return jax.shard_map(
        shards, mesh=fine, in_specs=placed, out_specs=P(CTX, CH), check_vma=False
    )
```

```python
import functools

import jax
import jax.numpy as jnp
from jax import lax
from jax.experimental import pallas as pl
from jax.experimental.pallas import tpu as pltpu
from jax.sharding import Mesh, PartitionSpec as P


CTX = ("x", "ylo", "core")
CH = ("yhi", "z")
FRONT = 256
BACK = 128
TALL = 16
LANES = 128
NT = (((1,), (1,)), ((), ()))
MIB = 1 << 20
WHOLE = pl.BlockSpec(memory_space=pltpu.VMEM)
FAR = pl.BlockSpec(memory_space=pltpu.HBM)
DMA = pltpu.SemaphoreType.DMA


def near(array):
    return pltpu.with_memory_space_constraint(array, pltpu.VMEM)


def far(array):
    return pltpu.with_memory_space_constraint(array, pltpu.HBM)


def params(mib):
    return pltpu.CompilerParams(vmem_limit_bytes=mib * MIB)


def places(shape, dimension):
    return lax.broadcasted_iota(jnp.int32, shape, dimension)


def identity(size):
    shape = (size, size)
    return (places(shape, 0) == places(shape, 1)).astype(jnp.bfloat16)


def ctx_index():
    return (lax.axis_index("x") * 2 + lax.axis_index("ylo")) * 2 + lax.axis_index("core")


def mix_kernel(key_ref, value_ref, out_ref, keys, values, sems):
    rows, width = keys.shape
    parts = out_ref.shape[0]
    pieces = 4
    step = width // pieces
    copies = []
    for n in range(pieces):
        at = pl.ds(n * step, step)
        pair = (
            pltpu.make_async_copy(key_ref.at[:, at], keys.at[:, at], sems.at[0, n]),
            pltpu.make_async_copy(value_ref.at[:, at], values.at[:, at], sems.at[1, n]),
        )
        for copy in pair:
            copy.start()
        copies.append(pair)
    unit = identity(step)
    own = width // parts
    for n, pair in enumerate(copies):
        for copy in pair:
            copy.wait()
        at = slice(n * step, (n + 1) * step)
        product = keys[:, at].astype(jnp.float32) * values[:, at].astype(jnp.float32)
        turned = lax.dot_general(
            unit, product.astype(jnp.bfloat16), NT, preferred_element_type=jnp.float32
        )
        turned = turned.astype(jnp.bfloat16).reshape(step // own, own, rows)
        here = slice(n * step // own, (n + 1) * step // own)
        out_ref[here, :own, :] = turned[:, :, :LANES]
        half = own // 2
        tail = turned[:, :, LANES:]
        out_ref[here, own:, :] = jnp.concatenate([tail[:, :half], tail[:, half:]], axis=2)


def mix(key_in, value_in, parts):
    rows, channels = key_in.shape
    return pl.pallas_call(
        mix_kernel,
        out_shape=pltpu.VMEM((parts, channels * rows // parts // LANES, LANES), jnp.bfloat16),
        in_specs=[FAR, FAR],
        out_specs=WHOLE,
        scratch_shapes=[
            pltpu.VMEM((rows, channels), jnp.bfloat16),
            pltpu.VMEM((rows, channels), jnp.bfloat16),
            DMA((2, 4)),
        ],
        compiler_params=params(6),
        name="mix",
    )(far(key_in), far(value_in))


def taps_kernel(filters_ref, out_ref, held, sem):
    fetch = pltpu.make_async_copy(filters_ref, held, sem)
    fetch.start()
    fetch.wait()
    groups = held.shape[0]
    own = out_ref.shape[0]
    base = ctx_index() * own

    @pl.loop(0, own)
    def _(g):
        pick = places((TALL, groups), 1) == base + g
        taps = jnp.dot(
            pick.astype(jnp.bfloat16), held[...], preferred_element_type=jnp.float32
        )
        front = jnp.zeros((TALL, FRONT), jnp.float32)
        line = jnp.concatenate([front, taps, jnp.zeros((TALL, BACK), jnp.float32)], axis=1)
        row = places(line.shape, 0)
        for bit in (1, 2, 4, 8):
            line = jnp.where((row & bit) != 0, pltpu.roll(line, bit, 1), line)
        for shift in range(8):
            moved = line if shift == 0 else pltpu.roll(line, TALL * shift, 1)
            out_ref[g, shift] = moved.astype(jnp.bfloat16)


def spread_taps(filters, parts):
    groups, seq = filters.shape
    own = groups // parts
    width = FRONT + seq + BACK
    return pl.pallas_call(
        taps_kernel,
        out_shape=pltpu.VMEM((own, 8, TALL, width), jnp.bfloat16),
        in_specs=[FAR],
        out_specs=WHOLE,
        scratch_shapes=[pltpu.VMEM(filters.shape, filters.dtype), DMA],
        compiler_params=params(8),
        cost_estimate=pl.CostEstimate(
            flops=2 * TALL * groups * seq * own, bytes_accessed=8 * MIB, transcendentals=0
        ),
        name="taps",
    )(far(filters))


def conv_kernel(x_ref, taps_ref, gain_ref, query_ref, out_ref, held_ref, acc_ref, gains, sems):
    first = pltpu.make_async_copy(gain_ref, gains, sems.at[0])
    fetch = pltpu.make_async_copy(query_ref, held_ref, sems.at[1])
    first.start()
    fetch.start()
    blocks = x_ref.shape[0]
    own, _, tall, _ = taps_ref.shape
    per_group = acc_ref.shape[0] // blocks
    channels = own * per_group
    rows = acc_ref.shape[1]
    base = ctx_index() * channels
    rest = rows - LANES

    @pl.loop(0, own // 2)
    def _(low):
        tails = []
        packed = x_ref[:, pl.ds(pl.multiple_of(channels + low * per_group, per_group), per_group), :]
        for high in range(2):
            g = high * 2 + low
            at = pl.multiple_of(g * per_group, per_group)
            piece = jnp.concatenate(
                [
                    x_ref[:, pl.ds(at, per_group), :],
                    packed[:, :, high * rest : (high + 1) * rest],
                ],
                axis=2,
            )
            acc_ref[...] = jnp.zeros_like(acc_ref)
            source = piece.reshape(blocks * per_group, rows)
            for lag in range(blocks):
                parts = []
                for k in range(rows // tall):
                    offset = FRONT + rows * lag - tall * k
                    shift = (-offset // tall) % 8
                    start = offset + tall * shift
                    parts.append(taps_ref[g, shift, :, start : start + rows])
                tile = jnp.concatenate(parts, axis=0)
                height = (blocks - lag) * per_group
                acc_ref[lag * per_group :, :] += jnp.dot(
                    source[:height], tile, preferred_element_type=jnp.float32
                )
            if high == 0:
                pl.when(low == 0)(first.wait)
            shape = (per_group, gains.shape[1])
            chosen = places(shape, 1) == base + at + places(shape, 0)
            gain = jnp.sum(jnp.where(chosen, gains[...], 0.0), axis=1, keepdims=True)
            total = acc_ref[...].reshape(blocks, per_group, rows)
            total = (total + piece.astype(jnp.float32) * gain[None]).astype(jnp.bfloat16)
            out_ref[:, pl.ds(at, per_group), :] = total[:, :, :LANES]
            tails.append(total[:, :, LANES:])
        here = pl.ds(pl.multiple_of(channels + low * per_group, per_group), per_group)
        out_ref[:, here, :] = jnp.concatenate(tails, axis=2)

    fetch.wait()


def convolve(x, taps, gain, query_in):
    blocks = x.shape[0]
    rows, channels = query_in.shape
    per_group = channels // blocks // taps.shape[0]
    return pl.pallas_call(
        conv_kernel,
        out_shape=(
            pltpu.VMEM(x.shape, jnp.bfloat16),
            pltpu.VMEM(query_in.shape, query_in.dtype),
        ),
        in_specs=[WHOLE, WHOLE, FAR, FAR],
        out_specs=(WHOLE, WHOLE),
        scratch_shapes=[
            pltpu.VMEM((blocks * per_group, rows), jnp.float32),
            pltpu.VMEM(gain.shape, gain.dtype),
            DMA((2,)),
        ],
        compiler_params=params(10),
        name="conv",
    )(near(x), near(taps), far(gain), far(query_in))


def gate_kernel(packed_ref, query_ref, out_ref):
    parts, _, _ = packed_ref.shape
    rows, width = query_ref.shape
    own = width // parts
    head = packed_ref[:, :own, :].reshape(width, LANES)
    tail = packed_ref[:, own:, :]
    tail = jnp.concatenate([tail, tail], axis=1).reshape(width, LANES)
    rest = rows - LANES
    upper = places(tail.shape, 0) // (own // 2) % 2
    tail = jnp.where(upper == places(tail.shape, 1) // rest, tail.astype(jnp.float32), 0.0)
    shape = (rest, LANES)
    fold = (places(shape, 1) % rest == places(shape, 0)).astype(jnp.bfloat16)
    for unit, turned, at in (
        (identity(LANES), head, slice(0, LANES)),
        (fold, tail.astype(jnp.bfloat16), slice(LANES, rows)),
    ):
        total = lax.dot_general(unit, turned, NT, preferred_element_type=jnp.float32)
        out_ref[at, :] = (query_ref[at, :].astype(jnp.float32) * total).astype(jnp.bfloat16)


def gate(packed, query_in):
    return pl.pallas_call(
        gate_kernel,
        out_shape=pltpu.VMEM(query_in.shape, jnp.bfloat16),
        in_specs=[WHOLE, WHOLE],
        out_specs=WHOLE,
        compiler_params=params(6),
        name="gate",
    )(near(packed), near(query_in))


def ring(size, step):
    return [(i, (i + step) % size) for i in range(size)]


def project_kernel(first, count, carried, *refs):
    refs = list(refs)
    blocks = [refs.pop(0) for _ in range(count)]
    slots = refs.pop(0)
    running = refs.pop(0) if carried else None
    (out_ref,) = refs
    width = out_ref.shape[1]
    tile = 256
    for m in range(0, width, tile):
        span = slice(m, m + tile)
        total = running[:, span] if carried else None
        for n, block in enumerate(blocks):
            part = jnp.dot(
                block[...], slots[first + n, :, span], preferred_element_type=jnp.float32
            )
            total = part if total is None else total + part
        out_ref[:, span] = total.astype(out_ref.dtype)


def project(first, blocks, slots, running, last):
    rows, depth = blocks[0].shape
    width = slots.shape[2]
    arrays = [near(block) for block in blocks] + [near(slots)]
    if running is not None:
        arrays.append(near(running))
    shape = (rows, width)
    return pl.pallas_call(
        functools.partial(project_kernel, first, len(blocks), running is not None),
        out_shape=(
            jax.ShapeDtypeStruct(shape, jnp.bfloat16) if last else pltpu.VMEM(shape, jnp.float32)
        ),
        in_specs=[WHOLE] * len(arrays),
        out_specs=WHOLE,
        compiler_params=params(4),
        cost_estimate=pl.CostEstimate(
            flops=2 * rows * depth * width * len(blocks),
            bytes_accessed=2 * depth * width * len(blocks),
            transcendentals=0,
        ),
        name="project",
    )(*arrays)


def fetch_kernel(weight_ref, slots_ref, sems):
    depth = slots_ref.shape[1]
    yhi, z = lax.axis_index("yhi"), lax.axis_index("z")
    pieces = sems.shape[1]
    step = depth // pieces
    copies = []
    for n, (side, back) in enumerate(OWNERS):
        owner = (yhi + side) % 2 * 4 + (z + 4 - back) % 4
        for m in range(pieces):
            at = pl.ds(pl.multiple_of(owner * depth + m * step, step), step)
            to = pl.ds(m * step, step)
            copies.append(
                pltpu.make_async_copy(weight_ref.at[at, :], slots_ref.at[n, to, :], sems.at[n, m])
            )
            copies[-1].start()
    for copy in copies:
        copy.wait()


def fetch(weight):
    count = len(OWNERS)
    shape = (count, weight.shape[0] // count, weight.shape[1])
    return pl.pallas_call(
        fetch_kernel,
        out_shape=pltpu.VMEM(shape, weight.dtype),
        in_specs=[FAR],
        out_specs=WHOLE,
        scratch_shapes=[DMA((count, 2))],
        compiler_params=params(2),
        cost_estimate=pl.CostEstimate(flops=0, bytes_accessed=2 * weight.size, transcendentals=0),
        name="fetch",
    )(far(weight))


def gather_project(gated, slots):
    def along(block, step):
        return lax.ppermute(block, "z", ring(4, step))

    def across(block):
        return lax.ppermute(block, "yhi", ring(2, 1))

    own = {2: along(gated, 2)}
    beyond = across(gated)
    own[1] = along(gated, 1)
    own[3] = along(gated, 3)
    other = {2: across(own[2])}
    other[1] = along(beyond, 1)
    other[3] = along(beyond, 3)
    total = project(0, [gated], slots, None, False)
    total = project(1, [own[2], beyond], slots, total, False)
    total = project(3, [own[1], own[3]], slots, total, False)
    total = project(5, [other[2]], slots, total, False)
    return project(6, [other[1], other[3]], slots, total, True)


def shards(query_in, key_in, value_in, filters, skip_gain, out_weight):
    parts = 16
    sent = mix(key_in, value_in, parts)
    whole = lax.all_to_all(sent, CTX, 0, 0, tiled=True)
    taps = spread_taps(filters, parts)
    slots = fetch(out_weight)
    total, query = convolve(whole, taps, skip_gain.reshape(1, -1), query_in)
    packed = lax.all_to_all(total, CTX, 0, 0, tiled=True)
    gated = gate(packed, query)
    return gather_project(gated, slots)


def solution(mesh):
    fine = Mesh(mesh.devices.reshape(4, 2, 2, 2, 4), CTX + CH)
    placed = (P(CTX, CH), P(CTX, CH), P(CTX, CH), P(CH, None), P(CH), P(None, CH))
    return jax.shard_map(
        shards, mesh=fine, in_specs=placed, out_specs=P(CTX, CH), check_vma=False
    )


OWNERS = ((0, 0), (0, 2), (1, 0), (0, 1), (0, 3), (1, 2), (1, 1), (1, 3))
```

```python
import functools

import jax
import jax.numpy as jnp
from jax import lax
from jax.experimental import pallas as pl
from jax.experimental.pallas import tpu as pltpu
from jax.sharding import Mesh, PartitionSpec as P


CTX = ("x", "ylo", "core")
CH = ("yhi", "z")
FRONT = 256
BACK = 128
TALL = 16
LANES = 128
QUAD = 4
NT = (((1,), (1,)), ((), ()))
MIB = 1 << 20
WHOLE = pl.BlockSpec(memory_space=pltpu.VMEM)
FAR = pl.BlockSpec(memory_space=pltpu.HBM)
DMA = pltpu.SemaphoreType.DMA


def near(array):
    return pltpu.with_memory_space_constraint(array, pltpu.VMEM)


def far(array):
    return pltpu.with_memory_space_constraint(array, pltpu.HBM)


def params(mib):
    return pltpu.CompilerParams(vmem_limit_bytes=mib * MIB)


def places(shape, dimension):
    return lax.broadcasted_iota(jnp.int32, shape, dimension)


def identity(size):
    shape = (size, size)
    return (places(shape, 0) == places(shape, 1)).astype(jnp.bfloat16)


def ctx_index():
    return (lax.axis_index("x") * 2 + lax.axis_index("ylo")) * 2 + lax.axis_index("core")


def mix_kernel(key_ref, value_ref, out_ref, keys, values, sems):
    rows, width = keys.shape
    parts = out_ref.shape[0]
    copies = (
        pltpu.make_async_copy(key_ref, keys, sems.at[0]),
        pltpu.make_async_copy(value_ref, values, sems.at[1]),
    )
    for copy in copies:
        copy.start()
    for copy in copies:
        copy.wait()
    step = 256
    unit = identity(step)
    own = width // parts
    half = own // 2
    for start in range(0, width, step):
        at = slice(start, start + step)
        product = keys[:, at].astype(jnp.float32) * values[:, at].astype(jnp.float32)
        turned = lax.dot_general(
            unit, product.astype(jnp.bfloat16), NT, preferred_element_type=jnp.float32
        )
        turned = turned.astype(jnp.bfloat16).reshape(step // own, own, rows)
        here = slice(start // own, (start + step) // own)
        out_ref[here, :own, :] = turned[:, :, :LANES]
        tail = turned[:, :, LANES:]
        out_ref[here, own:, :] = jnp.concatenate([tail[:, :half], tail[:, half:]], axis=2)


def mix(key_in, value_in, parts):
    rows, channels = key_in.shape
    return pl.pallas_call(
        mix_kernel,
        out_shape=pltpu.VMEM((parts, channels * rows // parts // LANES, LANES), jnp.bfloat16),
        in_specs=[FAR, FAR],
        out_specs=WHOLE,
        scratch_shapes=[
            pltpu.VMEM((rows, channels), jnp.bfloat16),
            pltpu.VMEM((rows, channels), jnp.bfloat16),
            DMA((2,)),
        ],
        compiler_params=params(6),
        name="mix",
    )(far(key_in), far(value_in))


def taps_kernel(filters_ref, out_ref, held, sem):
    fetch = pltpu.make_async_copy(filters_ref, held, sem)
    fetch.start()
    fetch.wait()
    groups = held.shape[0]
    own = out_ref.shape[0]
    base = ctx_index() * own

    @pl.loop(0, own)
    def _(g):
        pick = places((TALL, groups), 1) == base + g
        taps = jnp.dot(
            pick.astype(jnp.bfloat16), held[...], preferred_element_type=jnp.float32
        )
        front = jnp.zeros((TALL, FRONT), jnp.float32)
        line = jnp.concatenate([front, taps, jnp.zeros((TALL, BACK), jnp.float32)], axis=1)
        row = places(line.shape, 0)
        for bit in (1, 2, 4, 8):
            line = jnp.where((row & bit) != 0, pltpu.roll(line, bit, 1), line)
        for shift in range(8):
            moved = line if shift == 0 else pltpu.roll(line, TALL * shift, 1)
            out_ref[g, shift] = moved.astype(jnp.bfloat16)


def spread_taps(filters, parts):
    groups, seq = filters.shape
    own = groups // parts
    width = FRONT + seq + BACK
    return pl.pallas_call(
        taps_kernel,
        out_shape=pltpu.VMEM((own, 8, TALL, width), jnp.bfloat16),
        in_specs=[FAR],
        out_specs=WHOLE,
        scratch_shapes=[pltpu.VMEM(filters.shape, filters.dtype), DMA],
        compiler_params=params(8),
        cost_estimate=pl.CostEstimate(
            flops=2 * TALL * groups * seq * own, bytes_accessed=8 * MIB, transcendentals=0
        ),
        name="taps",
    )(far(filters))


def conv_kernel(
    far_ref, taps_ref, gain_ref, query_ref, out_ref, held_ref, acc_ref, x_ref, gains, sems
):
    arrive = pltpu.make_async_copy(far_ref, x_ref, sems.at[2])
    arrive.start()
    first = pltpu.make_async_copy(gain_ref, gains, sems.at[0])
    fetch = pltpu.make_async_copy(query_ref, held_ref, sems.at[1])
    first.start()
    fetch.start()
    blocks = x_ref.shape[0]
    own, _, tall, _ = taps_ref.shape
    per_group = acc_ref.shape[0] // blocks
    channels = own * per_group
    rows = acc_ref.shape[1]
    base = ctx_index() * channels
    rest = rows - LANES

    arrive.wait()
    for low in range(own // 2):
        tails = []
        packed = x_ref[:, pl.ds(channels + low * per_group, per_group), :]
        for high in range(2):
            g = high * 2 + low
            at = g * per_group
            piece = jnp.concatenate(
                [
                    x_ref[:, pl.ds(at, per_group), :],
                    packed[:, :, high * rest : (high + 1) * rest],
                ],
                axis=2,
            )
            lead = jnp.zeros(((QUAD - 1) * per_group, 2 * LANES), jnp.bfloat16)
            wide = jnp.concatenate(
                [piece, jnp.zeros((blocks, per_group, 2 * LANES - rows), jnp.bfloat16)], axis=2
            )
            source = jnp.concatenate([lead, wide.reshape(blocks * per_group, -1)], axis=0)
            blank = jnp.zeros((2 * LANES - rows, rows), jnp.bfloat16)
            for lag in range(0, blocks, QUAD):
                parts, shifted = [], []
                height = (blocks - lag) * per_group
                for step in range(QUAD):
                    for k in range(rows // tall):
                        offset = FRONT + rows * (lag + step) - tall * k
                        shift = (-offset // tall) % 8
                        start = offset + tall * shift
                        parts.append(taps_ref[g, shift, :, start : start + rows])
                    parts.append(blank)
                    top = (QUAD - 1 - step) * per_group
                    shifted.append(source[top : top + height])
                part = jnp.dot(
                    jnp.concatenate(shifted, axis=1),
                    jnp.concatenate(parts, axis=0),
                    preferred_element_type=jnp.float32,
                )
                if lag == 0:
                    acc_ref[...] = part
                else:
                    acc_ref[lag * per_group :, :] += part
            if g == 0:
                first.wait()
            shape = (per_group, gains.shape[1])
            chosen = places(shape, 1) == base + at + places(shape, 0)
            gain = jnp.sum(jnp.where(chosen, gains[...], 0.0), axis=1, keepdims=True)
            total = acc_ref[...].reshape(blocks, per_group, rows)
            total = (total + piece.astype(jnp.float32) * gain[None]).astype(jnp.bfloat16)
            out_ref[:, pl.ds(at, per_group), :] = total[:, :, :LANES]
            tails.append(total[:, :, LANES:])
        here = pl.ds(channels + low * per_group, per_group)
        out_ref[:, here, :] = jnp.concatenate(tails, axis=2)

    fetch.wait()


def convolve(x, taps, gain, query_in):
    blocks = x.shape[0]
    rows, channels = query_in.shape
    per_group = channels // blocks // taps.shape[0]
    return pl.pallas_call(
        conv_kernel,
        out_shape=(
            pltpu.VMEM(x.shape, jnp.bfloat16),
            pltpu.VMEM(query_in.shape, query_in.dtype),
        ),
        in_specs=[FAR, WHOLE, FAR, FAR],
        out_specs=(WHOLE, WHOLE),
        scratch_shapes=[
            pltpu.VMEM((blocks * per_group, rows), jnp.float32),
            pltpu.VMEM(x.shape, x.dtype),
            pltpu.VMEM(gain.shape, gain.dtype),
            DMA((3,)),
        ],
        compiler_params=params(10),
        name="conv",
    )(far(x), near(taps), far(gain), far(query_in))


def gate_kernel(packed_ref, query_ref, out_ref):
    parts, _, _ = packed_ref.shape
    rows, width = query_ref.shape
    own = width // parts
    head = packed_ref[:, :own, :].reshape(width, LANES)
    tail = packed_ref[:, own:, :]
    tail = jnp.concatenate([tail, tail], axis=1).reshape(width, LANES)
    rest = rows - LANES
    upper = places(tail.shape, 0) // (own // 2) % 2
    tail = jnp.where(upper == places(tail.shape, 1) // rest, tail.astype(jnp.float32), 0.0)
    shape = (rest, LANES)
    fold = (places(shape, 1) % rest == places(shape, 0)).astype(jnp.bfloat16)
    for unit, turned, at in (
        (identity(LANES), head, slice(0, LANES)),
        (fold, tail.astype(jnp.bfloat16), slice(LANES, rows)),
    ):
        total = lax.dot_general(unit, turned, NT, preferred_element_type=jnp.float32)
        out_ref[at, :] = (query_ref[at, :].astype(jnp.float32) * total).astype(jnp.bfloat16)


def gate(packed, query_in):
    return pl.pallas_call(
        gate_kernel,
        out_shape=pltpu.VMEM(query_in.shape, jnp.bfloat16),
        in_specs=[WHOLE, WHOLE],
        out_specs=WHOLE,
        compiler_params=params(6),
        name="gate",
    )(near(packed), near(query_in))


def ring(size, step):
    return [(i, (i + step) % size) for i in range(size)]


def project_kernel(first, count, carried, last, *refs):
    refs = list(refs)
    blocks = [refs.pop(0) for _ in range(count)]
    slots = refs.pop(0)
    running = refs.pop(0) if carried else None
    out_ref = refs.pop(0)
    width = out_ref.shape[1]
    tile = 256
    leaving = []
    for m in range(0, width, tile):
        span = slice(m, m + tile)
        total = running[:, span] if carried else None
        for n, block in enumerate(blocks):
            part = jnp.dot(
                block[...], slots[first + n, :, span], preferred_element_type=jnp.float32
            )
            total = part if total is None else total + part
        if not last:
            out_ref[:, span] = total
            continue
        held, sems = refs
        held[m // tile] = total.astype(held.dtype)
        leaving.append(
            pltpu.make_async_copy(
                held.at[m // tile], out_ref.at[:, pl.ds(m, tile)], sems.at[m // tile]
            )
        )
        leaving[-1].start()
    for copy in leaving:
        copy.wait()


def project(first, blocks, slots, running, last):
    rows, depth = blocks[0].shape
    width = slots.shape[2]
    arrays = [near(block) for block in blocks] + [near(slots)]
    if running is not None:
        arrays.append(near(running))
    shape = (rows, width)
    tiles = width // 256
    return pl.pallas_call(
        functools.partial(project_kernel, first, len(blocks), running is not None, last),
        out_shape=(
            jax.ShapeDtypeStruct(shape, jnp.bfloat16) if last else pltpu.VMEM(shape, jnp.float32)
        ),
        in_specs=[WHOLE] * len(arrays),
        out_specs=FAR if last else WHOLE,
        scratch_shapes=(
            [pltpu.VMEM((tiles, rows, 256), jnp.bfloat16), DMA((tiles,))] if last else []
        ),
        compiler_params=params(4),
        cost_estimate=pl.CostEstimate(
            flops=2 * rows * depth * width * len(blocks),
            bytes_accessed=2 * depth * width * len(blocks),
            transcendentals=0,
        ),
        name="project",
    )(*arrays)


def fetch_kernel(weight_ref, slots_ref, sems):
    depth = slots_ref.shape[1]
    yhi, z = lax.axis_index("yhi"), lax.axis_index("z")
    pieces = sems.shape[1]
    step = depth // pieces
    copies = []
    for n, (side, back) in enumerate(OWNERS):
        owner = (yhi + side) % 2 * 4 + (z + 4 - back) % 4
        for m in range(pieces):
            at = pl.ds(pl.multiple_of(owner * depth + m * step, step), step)
            to = pl.ds(m * step, step)
            copies.append(
                pltpu.make_async_copy(weight_ref.at[at, :], slots_ref.at[n, to, :], sems.at[n, m])
            )
            copies[-1].start()
    for copy in copies:
        copy.wait()


def fetch(weight):
    count = len(OWNERS)
    shape = (count, weight.shape[0] // count, weight.shape[1])
    return pl.pallas_call(
        fetch_kernel,
        out_shape=pltpu.VMEM(shape, weight.dtype),
        in_specs=[FAR],
        out_specs=WHOLE,
        scratch_shapes=[DMA((count, 2))],
        compiler_params=params(2),
        cost_estimate=pl.CostEstimate(flops=0, bytes_accessed=2 * weight.size, transcendentals=0),
        name="fetch",
    )(far(weight))


def gather_project(gated, slots):
    def along(block, step):
        return lax.ppermute(block, "z", ring(4, step))

    def across(block):
        return lax.ppermute(block, "yhi", ring(2, 1))

    own = {2: along(gated, 2)}
    beyond = across(gated)
    own[1] = along(gated, 1)
    own[3] = along(gated, 3)
    other = {2: across(own[2])}
    other[1] = along(beyond, 1)
    other[3] = along(beyond, 3)
    total = project(0, [gated], slots, None, False)
    total = project(1, [own[2], beyond], slots, total, False)
    total = project(3, [own[1], own[3]], slots, total, False)
    total = project(5, [other[2]], slots, total, False)
    return project(6, [other[1], other[3]], slots, total, True)


def shards(query_in, key_in, value_in, filters, skip_gain, out_weight):
    parts = 16
    sent = mix(key_in, value_in, parts)
    whole = lax.all_to_all(sent, CTX, 0, 0, tiled=True)
    taps = spread_taps(filters, parts)
    slots = fetch(out_weight)
    total, query = convolve(whole, taps, skip_gain.reshape(1, -1), query_in)
    packed = lax.all_to_all(total, CTX, 0, 0, tiled=True)
    gated = gate(packed, query)
    return gather_project(gated, slots)


def solution(mesh):
    fine = Mesh(mesh.devices.reshape(4, 2, 2, 2, 4), CTX + CH)
    placed = (P(CTX, CH), P(CTX, CH), P(CTX, CH), P(CH, None), P(CH), P(None, CH))
    return jax.shard_map(
        shards, mesh=fine, in_specs=placed, out_specs=P(CTX, CH), check_vma=False
    )


OWNERS = ((0, 0), (0, 2), (1, 0), (0, 1), (0, 3), (1, 2), (1, 1), (1, 3))
```

```python
import functools

import jax
import jax.numpy as jnp
from jax import lax
from jax.experimental import pallas as pl
from jax.experimental.pallas import tpu as pltpu
from jax.sharding import Mesh, PartitionSpec as P


CTX = ("x", "ylo", "core")
CH = ("yhi", "z")
FRONT = 256
BACK = 128
TALL = 16
LANES = 128
QUAD = 4
NT = (((1,), (1,)), ((), ()))
MIB = 1 << 20
WHOLE = pl.BlockSpec(memory_space=pltpu.VMEM)
FAR = pl.BlockSpec(memory_space=pltpu.HBM)
DMA = pltpu.SemaphoreType.DMA


def near(array):
    return pltpu.with_memory_space_constraint(array, pltpu.VMEM)


def far(array):
    return pltpu.with_memory_space_constraint(array, pltpu.HBM)


def params(mib):
    return pltpu.CompilerParams(vmem_limit_bytes=mib * MIB)


def places(shape, dimension):
    return lax.broadcasted_iota(jnp.int32, shape, dimension)


def identity(size):
    shape = (size, size)
    return (places(shape, 0) == places(shape, 1)).astype(jnp.bfloat16)


def ctx_index():
    return (lax.axis_index("x") * 2 + lax.axis_index("ylo")) * 2 + lax.axis_index("core")


def mix_kernel(key_ref, value_ref, out_ref, keys, values, sems):
    rows, width = keys.shape
    parts = out_ref.shape[0]
    copies = (
        pltpu.make_async_copy(key_ref, keys, sems.at[0]),
        pltpu.make_async_copy(value_ref, values, sems.at[1]),
    )
    for copy in copies:
        copy.start()
    for copy in copies:
        copy.wait()
    step = 256
    unit = identity(step)
    own = width // parts
    half = own // 2
    for start in range(0, width, step):
        at = slice(start, start + step)
        product = keys[:, at].astype(jnp.float32) * values[:, at].astype(jnp.float32)
        turned = lax.dot_general(
            unit, product.astype(jnp.bfloat16), NT, preferred_element_type=jnp.float32
        )
        turned = turned.astype(jnp.bfloat16).reshape(step // own, own, rows)
        here = slice(start // own, (start + step) // own)
        out_ref[here, :own, :] = turned[:, :, :LANES]
        tail = turned[:, :, LANES:]
        out_ref[here, own:, :] = jnp.concatenate([tail[:, :half], tail[:, half:]], axis=2)


def mix(key_in, value_in, parts):
    rows, channels = key_in.shape
    return pl.pallas_call(
        mix_kernel,
        out_shape=pltpu.VMEM((parts, channels * rows // parts // LANES, LANES), jnp.bfloat16),
        in_specs=[FAR, FAR],
        out_specs=WHOLE,
        scratch_shapes=[
            pltpu.VMEM((rows, channels), jnp.bfloat16),
            pltpu.VMEM((rows, channels), jnp.bfloat16),
            DMA((2,)),
        ],
        compiler_params=params(6),
        name="mix",
    )(far(key_in), far(value_in))


def taps_kernel(filters_ref, out_ref, held, sem):
    fetch = pltpu.make_async_copy(filters_ref, held, sem)
    fetch.start()
    fetch.wait()
    groups = held.shape[0]
    own = out_ref.shape[0]
    base = ctx_index() * own

    @pl.loop(0, own)
    def _(g):
        pick = places((TALL, groups), 1) == base + g
        taps = jnp.dot(
            pick.astype(jnp.bfloat16), held[...], preferred_element_type=jnp.float32
        )
        front = jnp.zeros((TALL, FRONT), jnp.float32)
        line = jnp.concatenate([front, taps, jnp.zeros((TALL, BACK), jnp.float32)], axis=1)
        row = places(line.shape, 0)
        for bit in (1, 2, 4, 8):
            line = jnp.where((row & bit) != 0, pltpu.roll(line, bit, 1), line)
        for shift in range(8):
            moved = line if shift == 0 else pltpu.roll(line, TALL * shift, 1)
            out_ref[g, shift] = moved.astype(jnp.bfloat16)


def spread_taps(filters, parts):
    groups, seq = filters.shape
    own = groups // parts
    width = FRONT + seq + BACK
    return pl.pallas_call(
        taps_kernel,
        out_shape=pltpu.VMEM((own, 8, TALL, width), jnp.bfloat16),
        in_specs=[FAR],
        out_specs=WHOLE,
        scratch_shapes=[pltpu.VMEM(filters.shape, filters.dtype), DMA],
        compiler_params=params(8),
        cost_estimate=pl.CostEstimate(
            flops=2 * TALL * groups * seq * own, bytes_accessed=8 * MIB, transcendentals=0
        ),
        name="taps",
    )(far(filters))


def conv_kernel(x_ref, taps_ref, gain_ref, query_ref, out_ref, held_ref, acc_ref, gains, sems):
    first = pltpu.make_async_copy(gain_ref, gains, sems.at[0])
    fetch = pltpu.make_async_copy(query_ref, held_ref, sems.at[1])
    first.start()
    fetch.start()
    blocks = x_ref.shape[0]
    own, _, tall, _ = taps_ref.shape
    per_group = acc_ref.shape[0] // blocks
    channels = own * per_group
    rows = acc_ref.shape[1]
    base = ctx_index() * channels
    rest = rows - LANES

    for low in range(own // 2):
        tails = []
        packed = x_ref[:, pl.ds(channels + low * per_group, per_group), :]
        for high in range(2):
            g = high * 2 + low
            at = g * per_group
            piece = jnp.concatenate(
                [
                    x_ref[:, pl.ds(at, per_group), :],
                    packed[:, :, high * rest : (high + 1) * rest],
                ],
                axis=2,
            )
            lead = jnp.zeros(((QUAD - 1) * per_group, 2 * LANES), jnp.bfloat16)
            wide = jnp.concatenate(
                [piece, jnp.zeros((blocks, per_group, 2 * LANES - rows), jnp.bfloat16)], axis=2
            )
            source = jnp.concatenate([lead, wide.reshape(blocks * per_group, -1)], axis=0)
            blank = jnp.zeros((2 * LANES - rows, rows), jnp.bfloat16)
            for lag in range(0, blocks, QUAD):
                parts, shifted = [], []
                height = (blocks - lag) * per_group
                for step in range(QUAD):
                    for k in range(rows // tall):
                        offset = FRONT + rows * (lag + step) - tall * k
                        shift = (-offset // tall) % 8
                        start = offset + tall * shift
                        parts.append(taps_ref[g, shift, :, start : start + rows])
                    parts.append(blank)
                    top = (QUAD - 1 - step) * per_group
                    shifted.append(source[top : top + height])
                part = jnp.dot(
                    jnp.concatenate(shifted, axis=1),
                    jnp.concatenate(parts, axis=0),
                    preferred_element_type=jnp.float32,
                )
                if lag == 0:
                    acc_ref[...] = part
                else:
                    acc_ref[lag * per_group :, :] += part
            if g == 0:
                first.wait()
            shape = (per_group, gains.shape[1])
            chosen = places(shape, 1) == base + at + places(shape, 0)
            gain = jnp.sum(jnp.where(chosen, gains[...], 0.0), axis=1, keepdims=True)
            total = acc_ref[...].reshape(blocks, per_group, rows)
            total = (total + piece.astype(jnp.float32) * gain[None]).astype(jnp.bfloat16)
            out_ref[:, pl.ds(at, per_group), :] = total[:, :, :LANES]
            tails.append(total[:, :, LANES:])
        here = pl.ds(channels + low * per_group, per_group)
        out_ref[:, here, :] = jnp.concatenate(tails, axis=2)

    fetch.wait()


def convolve(x, taps, gain, query_in):
    blocks = x.shape[0]
    rows, channels = query_in.shape
    per_group = channels // blocks // taps.shape[0]
    return pl.pallas_call(
        conv_kernel,
        out_shape=(
            pltpu.VMEM(x.shape, jnp.bfloat16),
            pltpu.VMEM(query_in.shape, query_in.dtype),
        ),
        in_specs=[WHOLE, WHOLE, FAR, FAR],
        out_specs=(WHOLE, WHOLE),
        scratch_shapes=[
            pltpu.VMEM((blocks * per_group, rows), jnp.float32),
            pltpu.VMEM(gain.shape, gain.dtype),
            DMA((2,)),
        ],
        compiler_params=params(10),
        name="conv",
    )(near(x), near(taps), far(gain), far(query_in))


def gate_kernel(packed_ref, query_ref, out_ref):
    parts, _, _ = packed_ref.shape
    rows, width = query_ref.shape
    own = width // parts
    head = packed_ref[:, :own, :].reshape(width, LANES)
    tail = packed_ref[:, own:, :]
    tail = jnp.concatenate([tail, tail], axis=1).reshape(width, LANES)
    rest = rows - LANES
    upper = places(tail.shape, 0) // (own // 2) % 2
    tail = jnp.where(upper == places(tail.shape, 1) // rest, tail.astype(jnp.float32), 0.0)
    shape = (rest, LANES)
    fold = (places(shape, 1) % rest == places(shape, 0)).astype(jnp.bfloat16)
    for unit, turned, at in (
        (identity(LANES), head, slice(0, LANES)),
        (fold, tail.astype(jnp.bfloat16), slice(LANES, rows)),
    ):
        total = lax.dot_general(unit, turned, NT, preferred_element_type=jnp.float32)
        out_ref[at, :] = (query_ref[at, :].astype(jnp.float32) * total).astype(jnp.bfloat16)


def gate(packed, query_in):
    return pl.pallas_call(
        gate_kernel,
        out_shape=pltpu.VMEM(query_in.shape, jnp.bfloat16),
        in_specs=[WHOLE, WHOLE],
        out_specs=WHOLE,
        compiler_params=params(6),
        name="gate",
    )(near(packed), near(query_in))


def ring(size, step):
    return [(i, (i + step) % size) for i in range(size)]


def project_kernel(first, count, carried, last, *refs):
    refs = list(refs)
    blocks = [refs.pop(0) for _ in range(count)]
    slots = refs.pop(0)
    running = refs.pop(0) if carried else None
    out_ref = refs.pop(0)
    width = out_ref.shape[1]
    tile = 256
    leaving = []
    for m in range(0, width, tile):
        span = slice(m, m + tile)
        total = running[:, span] if carried else None
        for n, block in enumerate(blocks):
            part = jnp.dot(
                block[...], slots[first + n, :, span], preferred_element_type=jnp.float32
            )
            total = part if total is None else total + part
        if not last:
            out_ref[:, span] = total
            continue
        held, sems = refs
        held[m // tile] = total.astype(held.dtype)
        leaving.append(
            pltpu.make_async_copy(
                held.at[m // tile], out_ref.at[:, pl.ds(m, tile)], sems.at[m // tile]
            )
        )
        leaving[-1].start()
    for copy in leaving:
        copy.wait()


def project(first, blocks, slots, running, last):
    rows, depth = blocks[0].shape
    width = slots.shape[2]
    arrays = [near(block) for block in blocks] + [near(slots)]
    if running is not None:
        arrays.append(near(running))
    shape = (rows, width)
    tiles = width // 256
    return pl.pallas_call(
        functools.partial(project_kernel, first, len(blocks), running is not None, last),
        out_shape=(
            jax.ShapeDtypeStruct(shape, jnp.bfloat16) if last else pltpu.VMEM(shape, jnp.float32)
        ),
        in_specs=[WHOLE] * len(arrays),
        out_specs=FAR if last else WHOLE,
        scratch_shapes=(
            [pltpu.VMEM((tiles, rows, 256), jnp.bfloat16), DMA((tiles,))] if last else []
        ),
        compiler_params=params(4),
        cost_estimate=pl.CostEstimate(
            flops=2 * rows * depth * width * len(blocks),
            bytes_accessed=2 * depth * width * len(blocks),
            transcendentals=0,
        ),
        name="project",
    )(*arrays)


def fetch_kernel(weight_ref, slots_ref, sems):
    depth = slots_ref.shape[1]
    yhi, z = lax.axis_index("yhi"), lax.axis_index("z")
    pieces = sems.shape[1]
    step = depth // pieces
    copies = []
    for n, (side, back) in enumerate(OWNERS):
        owner = (yhi + side) % 2 * 4 + (z + 4 - back) % 4
        for m in range(pieces):
            at = pl.ds(pl.multiple_of(owner * depth + m * step, step), step)
            to = pl.ds(m * step, step)
            copies.append(
                pltpu.make_async_copy(weight_ref.at[at, :], slots_ref.at[n, to, :], sems.at[n, m])
            )
            copies[-1].start()
    for copy in copies:
        copy.wait()


def fetch(weight):
    count = len(OWNERS)
    shape = (count, weight.shape[0] // count, weight.shape[1])
    return pl.pallas_call(
        fetch_kernel,
        out_shape=pltpu.VMEM(shape, weight.dtype),
        in_specs=[FAR],
        out_specs=WHOLE,
        scratch_shapes=[DMA((count, 2))],
        compiler_params=params(2),
        cost_estimate=pl.CostEstimate(flops=0, bytes_accessed=2 * weight.size, transcendentals=0),
        name="fetch",
    )(far(weight))


def gather_project(gated, slots):
    def along(block, step):
        return lax.ppermute(block, "z", ring(4, step))

    def across(block):
        return lax.ppermute(block, "yhi", ring(2, 1))

    own = {2: along(gated, 2)}
    beyond = across(gated)
    own[1] = along(gated, 1)
    own[3] = along(gated, 3)
    other = {2: across(own[2])}
    other[1] = along(beyond, 1)
    other[3] = along(beyond, 3)
    total = project(0, [gated], slots, None, False)
    total = project(1, [own[2], beyond], slots, total, False)
    total = project(3, [own[1], own[3]], slots, total, False)
    total = project(5, [other[2]], slots, total, False)
    return project(6, [other[1], other[3]], slots, total, True)


def shards(query_in, key_in, value_in, filters, skip_gain, out_weight):
    parts = 16
    sent = mix(key_in, value_in, parts)
    whole = lax.all_to_all(sent, CTX, 0, 0, tiled=True)
    taps = spread_taps(filters, parts)
    slots = fetch(out_weight)
    total, query = convolve(whole, taps, skip_gain.reshape(1, -1), query_in)
    packed = lax.all_to_all(total, CTX, 0, 0, tiled=True)
    gated = gate(packed, query)
    return gather_project(gated, slots)


def solution(mesh):
    fine = Mesh(mesh.devices.reshape(4, 2, 2, 2, 4), CTX + CH)
    placed = (P(CTX, CH), P(CTX, CH), P(CTX, CH), P(CH, None), P(CH), P(None, CH))
    return jax.shard_map(
        shards, mesh=fine, in_specs=placed, out_specs=P(CTX, CH), check_vma=False
    )


OWNERS = ((0, 0), (0, 2), (1, 0), (0, 1), (0, 3), (1, 2), (1, 1), (1, 3))
```
